32 devices in a mesh: sample: 2 (over x), row: 16 (over z, y, core).
Axes of the slice: x: 2, y: 2, z: 4, core: 2. Of those that a mesh axis runs over, the one named last changes fastest.
Arguments:
- atom_single: bfloat16 [16384, 128], P(('sample', 'row')), parts along dimension 0, may hold values from -6 to 6
- atom_count: int32 [16], replicated, may hold values from 128 to 512, as said below
- atom_token: int32 [8192], P('row'), may hold values from 0 to 63, as said below
- atom_bias: bfloat16 [256, 4, 32, 128], P('row'), may hold values from -4 to 236
- token_single: bfloat16 [2048, 768], P(('sample', 'row')), parts along dimension 0, may hold values from -6 to 6
- token_bias: bfloat16 [16, 1024, 1024], P(None, 'row'), may hold values from -4 to 236
- atom_gain: float32 [128], replicated, may hold values from 0.25 to 1.75
- atom_qkvg: bfloat16 [128, 512], replicated, may hold values from -0.5 to 0.5
- atom_proj: bfloat16 [128, 128], replicated, may hold values from -0.5 to 0.5
- atom_to_token: bfloat16 [128, 768], replicated, may hold values from -0.5 to 0.5
- token_gain: float32 [768], replicated, may hold values from 0.25 to 1.75
- token_qg: bfloat16 [768, 1536], replicated, may hold values from -0.21875 to 0.21875
- token_kv: bfloat16 [768, 1536], replicated, may hold values from -0.21875 to 0.21875
- token_proj: bfloat16 [768, 768], replicated, may hold values from -0.21875 to 0.21875
- token_to_atom: bfloat16 [768, 128], replicated, may hold values from -0.21875 to 0.21875
Outputs:
- atom_out: bfloat16 [16384, 128], P(('sample', 'row')), parts along dimension 0
- token_out: bfloat16 [2048, 768], P(('sample', 'row')), parts along dimension 0
The draws below stay inside these ranges and needn't reach their ends.
There are 2 independent parts, one for each index of `sample`. The reference program is written for one: setup_inputs(seed, part) draws one part's arguments, and reference() takes and returns one part's arrays. A program takes and returns all parts, laid end to end along the dimension named above; an argument that names none is the same for every part. Nothing has to cross between parts.
Inputs may be any that keep to these rules, and one draw needn't show every extreme that they name: `atom_count`: entry b counts the live slots of atoms b * 512 to (b + 1) * 512 - 1, which are the first ones of that block; some block has exactly 512 and another exactly 128. `atom_token`: within a block of 512 slots the live slots' values never fall and each of the 64 values occurs in at least one live slot; slots that are not live hold 0.
All inputs are finite; a program needn't handle non-finite values.
Results may differ from the reference program's by a relative error of at most 0.0051.
Values may be sent and summed in bfloat16 or wider, within the bound.
No kernel may reach another device: no remote copies, remote signals or barrier semaphores. Data moves between devices by JAX's collectives and lax.ppermute only.
A program may use at most 128 MiB of HBM per device.

```python
import jax
import jax.numpy as jnp
from jax import lax

TW = 768
TH = 16
AW = 128
AH = 4
WQ = 32
WK = 128
TOK_DEV = 64
ATOM_DEV = 512
LEFT_RIM = 48
RIGHT_RIM = 80
N_TOK = 1024
ATOMS = 8192
BLOCKS = 256
N_ROW = 16


def layout(key):
    base = jax.random.fold_in(key, 101)
    streams = jax.random.split(base, 6)
    ligand = jax.random.randint(streams[0], (N_ROW,), 0, 4) == 0
    lowest = ATOM_DEV // 4
    heavy = jax.random.randint(streams[1], (N_ROW,), 5 * ATOM_DEV // 8, ATOM_DEV + 1)
    light = jax.random.randint(streams[2], (N_ROW,), lowest, 3 * ATOM_DEV // 8)
    counts = jnp.where(ligand, light, heavy)
    fullest = jax.random.randint(streams[3], (), 0, N_ROW)
    emptiest = (fullest + 1 + jax.random.randint(streams[4], (), 0, N_ROW - 1)) % N_ROW
    counts = counts.at[fullest].set(ATOM_DEV).at[emptiest].set(lowest)
    slots = jnp.arange(ATOM_DEV, dtype=jnp.int32)
    ranking = jax.random.randint(streams[5], (N_ROW, ATOM_DEV), 0, 2 ** 18)
    allowed = (slots[None, :] >= 1) & (slots[None, :] < counts[:, None])
    ranked = jnp.where(allowed, ranking * ATOM_DEV + slots[None, :], -1)
    chosen = lax.top_k(ranked, TOK_DEV - 1)[0]
    cuts = chosen % ATOM_DEV
    tokens = jnp.sum((cuts[:, None, :] <= slots[None, :, None]).astype(jnp.int32), axis=2)
    tokens = jnp.where(slots[None, :] < counts[:, None], tokens, 0)
    return (counts.astype(jnp.int32), tokens.reshape(N_ROW * ATOM_DEV).astype(jnp.int32))


def draw_atom_count(key, part):
    return layout(key)[0]


def draw_atom_token(key, part):
    return layout(key)[1]


def background(key, shape):
    return jnp.clip(jax.random.normal(key, shape, jnp.float32), -4.0, 4.0)


def draw_token_bias(key, part):
    streams = jax.random.split(jax.random.fold_in(key, 211), 1)
    values = background(streams[0], (TH, N_TOK, N_TOK))
    return values.astype(jnp.bfloat16)


def draw_atom_bias(key, part):
    streams = jax.random.split(jax.random.fold_in(key, 307), 1)
    values = background(streams[0], (BLOCKS, AH, WQ, WK))
    return values.astype(jnp.bfloat16)


def steps_of(stream_key, dims, pieces, low, top_value):
    level = 1.0
    for axis_at, blocks in pieces:
        heights = jax.random.uniform(jax.random.fold_in(jax.random.fold_in(stream_key, 6), axis_at), (blocks,), jnp.float32, low / len(pieces), top_value / len(pieces))
        level = level * jnp.repeat(jnp.exp(heights), dims[axis_at] // blocks).reshape((-1,) + (1,) * (len(dims) - 1 - axis_at))
    return level


def normal_values(stream_key, shape, scale, reach, shards=(), held_as=jnp.bfloat16):
    values = scale * jax.random.normal(stream_key, shape, jnp.float32)
    if shards:
        values = values * steps_of(stream_key, shape, shards, -0.22, 0.18)
    return jnp.clip(values, -reach, reach).astype(held_as)


def setup_inputs(seed: int = 0, part: int = 0) -> dict:
    key_of = jax.random.split(jax.random.key(seed), 16)
    part_splits = jax.random.split(jax.random.fold_in(key_of[15], part), 16)
    return {
        "atom_single": normal_values(part_splits[0], (ATOMS, AW), 1.0, 6.0, ((0, 16),)),
        "atom_count": draw_atom_count(jax.random.fold_in(key_of[15], 71), part),
        "atom_token": draw_atom_token(jax.random.fold_in(key_of[15], 71), part),
        "atom_bias": draw_atom_bias(jax.random.fold_in(key_of[15], 71), part),
        "token_single": normal_values(part_splits[4], (N_TOK, TW), 1.0, 6.0, ((0, 16),)),
        "token_bias": draw_token_bias(jax.random.fold_in(key_of[15], 71), part),
        "atom_gain": jnp.clip(1.0 + 0.15 * jax.random.normal(key_of[6], (AW,), jnp.float32), 0.25, 1.75),
        "atom_qkvg": normal_values(key_of[7], (AW, 4 * AW), AW ** -0.5, 0.5),
        "atom_proj": normal_values(key_of[8], (AW, AW), AW ** -0.5, 0.5),
        "atom_to_token": normal_values(key_of[9], (AW, TW), AW ** -0.5, 0.5),
        "token_gain": jnp.clip(1.0 + 0.15 * jax.random.normal(key_of[10], (TW,), jnp.float32), 0.25, 1.75),
        "token_qg": normal_values(key_of[11], (TW, 2 * TW), TW ** -0.5, 0.21875),
        "token_kv": normal_values(key_of[12], (TW, 2 * TW), TW ** -0.5, 0.21875),
        "token_proj": normal_values(key_of[13], (TW, TW), TW ** -0.5, 0.21875),
        "token_to_atom": normal_values(key_of[14], (TW, AW), TW ** -0.5, 0.21875),
    }


EPSILON = 1e-05
MASKED = -1000000000.0

def layer_norm(values, gain):
    floats = values.astype(jnp.float32)
    average = lax.optimization_barrier(jnp.mean(floats, axis=-1, keepdims=True))
    centred = floats - average
    spread = lax.optimization_barrier(jnp.mean(centred * centred, axis=-1, keepdims=True))
    return (centred * lax.rsqrt(spread + EPSILON) * gain).astype(jnp.bfloat16)

def window_attention(projected, before, after_rim, live_count, bias_block, is_first, is_last):
    blocks = ATOM_DEV // WQ
    head_size = AW // AH
    queries = projected[:, :AW].reshape(blocks, WQ, AH, head_size).astype(jnp.float32)
    keyval = projected[:, AW:3 * AW]
    extended = jnp.concatenate([before, keyval, jnp.zeros((RIGHT_RIM, 2 * AW), keyval.dtype)], axis=0)
    extended = lax.dynamic_update_slice_in_dim(extended, after_rim, (LEFT_RIM + live_count).astype(jnp.int32), 0)
    tile_rows = extended.reshape(blocks + WK // WQ, WQ, 2 * AW)
    windows = jnp.concatenate([tile_rows[offset_block:offset_block + blocks] for offset_block in range(WK // WQ)], axis=1)
    key_rows = windows[:, :, :AW].reshape(blocks, WK, AH, head_size).astype(jnp.float32)
    value_rows = windows[:, :, AW:].reshape(blocks, WK, AH, head_size).astype(jnp.float32)
    scores = jnp.einsum('bqhd,bkhd->bhqk', queries, key_rows) * head_size ** (-0.5) + bias_block.astype(jnp.float32)
    places = WQ * jnp.arange(blocks, dtype=jnp.int32)[:, None] - LEFT_RIM + jnp.arange(WK, dtype=jnp.int32)[None, :]
    usable = ((places >= 0) | jnp.logical_not(is_first)) & ((places < live_count) | jnp.logical_not(is_last))
    scores = jnp.where(usable[:, None, None, :], scores, MASKED)
    row_max = lax.optimization_barrier(jnp.max(scores, axis=-1, keepdims=True))
    raised = jnp.exp(scores - row_max)
    totals = lax.optimization_barrier(jnp.sum(raised, axis=-1))
    weights = raised.astype(jnp.bfloat16).astype(jnp.float32)
    attended = jnp.einsum('bhqk,bkhd->bqhd', weights, value_rows) / jnp.transpose(totals, (0, 2, 1))[:, :, :, None]
    return attended.reshape(ATOM_DEV, AW)

def reference(atom_single, atom_count, atom_token, atom_bias, token_single, token_bias, atom_gain, atom_qkvg, atom_proj, atom_to_token, token_gain, token_qg, token_kv, token_proj, token_to_atom):
    normed = layer_norm(atom_single, atom_gain)
    projected = jnp.dot(normed, atom_qkvg, preferred_element_type=jnp.float32).astype(jnp.bfloat16)
    projected = projected.reshape(N_ROW, ATOM_DEV, 4 * AW)
    keyval = projected[:, :, AW:3 * AW]
    tails = jax.vmap(lambda rows, number: lax.dynamic_slice_in_dim(rows, (number - LEFT_RIM).astype(jnp.int32), LEFT_RIM, 0))(keyval, atom_count)
    heads = keyval[:, :RIGHT_RIM]
    before = jnp.concatenate([jnp.zeros((1, LEFT_RIM, 2 * AW), keyval.dtype), tails[:-1]], axis=0)
    after_rim = jnp.concatenate([heads[1:], jnp.zeros((1, RIGHT_RIM, 2 * AW), keyval.dtype)], axis=0)
    bias_blocks = atom_bias.reshape(N_ROW, ATOM_DEV // WQ, AH, WQ, WK)
    devices = jnp.arange(N_ROW, dtype=jnp.int32)

    def per_device(items):
        rows, prior, later, number, bias_block, device_no = items
        return window_attention(rows, prior, later, number, bias_block, device_no == 0, device_no == N_ROW - 1)
    attended = lax.map(per_device, (projected, before, after_rim, atom_count, bias_blocks, devices))
    gate_part = projected[:, :, 3 * AW:].astype(jnp.float32)
    gated = (attended * jax.nn.sigmoid(gate_part)).astype(jnp.bfloat16).reshape(ATOMS, AW)
    atom_mid = (atom_single.astype(jnp.float32) + jnp.dot(gated, atom_proj, preferred_element_type=jnp.float32)).astype(jnp.bfloat16)
    offsets = jnp.arange(ATOM_DEV, dtype=jnp.int32)
    is_live = (offsets[None, :] < atom_count[:, None]).reshape(ATOMS)
    lifted = jax.nn.relu(jnp.dot(atom_mid, atom_to_token, preferred_element_type=jnp.float32)).astype(jnp.bfloat16)
    owner = (jnp.repeat(devices, ATOM_DEV) * TOK_DEV + atom_token).astype(jnp.int32)
    live_weight = is_live.astype(jnp.float32)
    summed = jax.ops.segment_sum(lifted.astype(jnp.float32) * live_weight[:, None], owner, num_segments=N_TOK)
    counts = jax.ops.segment_sum(live_weight, owner, num_segments=N_TOK)
    pooled = summed / counts[:, None]
    hidden = token_single.astype(jnp.float32) + pooled
    normed_tok = layer_norm(hidden, token_gain)
    query_gate = jnp.dot(normed_tok, token_qg, preferred_element_type=jnp.float32).astype(jnp.bfloat16)
    keyval_tok = jnp.dot(normed_tok, token_kv, preferred_element_type=jnp.float32).astype(jnp.bfloat16)
    head_size = TW // TH
    key_rows = keyval_tok[:, :TW].reshape(N_TOK, TH, head_size).astype(jnp.float32)
    value_rows = keyval_tok[:, TW:].reshape(N_TOK, TH, head_size).astype(jnp.float32)
    queries_all = query_gate[:, :TW].reshape(N_TOK, TH, head_size)

    def attend(device_no):
        queries = lax.dynamic_slice_in_dim(queries_all, device_no * TOK_DEV, TOK_DEV, 0).astype(jnp.float32)
        bias_tile = lax.dynamic_slice_in_dim(token_bias, device_no * TOK_DEV, TOK_DEV, 1).astype(jnp.float32)
        scores = jnp.einsum('qhd,khd->hqk', queries, key_rows) * head_size ** (-0.5) + bias_tile
        row_max = lax.optimization_barrier(jnp.max(scores, axis=-1, keepdims=True))
        raised = jnp.exp(scores - row_max)
        totals = lax.optimization_barrier(jnp.sum(raised, axis=-1))
        weights = raised.astype(jnp.bfloat16).astype(jnp.float32)
        result = jnp.einsum('hqk,khd->qhd', weights, value_rows) / jnp.transpose(totals)[:, :, None]
        return result.reshape(TOK_DEV, TW)
    attended_tok = lax.map(attend, devices).reshape(N_TOK, TW)
    gated_tok = (attended_tok * jax.nn.sigmoid(query_gate[:, TW:].astype(jnp.float32))).astype(jnp.bfloat16)
    token_out = (hidden + jnp.dot(gated_tok, token_proj, preferred_element_type=jnp.float32)).astype(jnp.bfloat16)
    lifted_back = jnp.dot(token_out, token_to_atom, preferred_element_type=jnp.float32)
    atom_out = jnp.where(is_live[:, None], atom_mid.astype(jnp.float32) + jnp.take(lifted_back, owner, axis=0), 0.0).astype(jnp.bfloat16)
    return (atom_out, token_out)
```

```python
import jax
import jax.numpy as jnp
from jax import lax
from jax.experimental import pallas as pl
from jax.experimental.pallas import tpu as pltpu
from jax.sharding import PartitionSpec as P

TW = 768
TH = 16
AW = 128
AH = 4
WQ = 32
WK = 128
LEFT_RIM = 48
RIGHT_RIM = 80
AD = AW // AH
TD = TW // TH

EPSILON = 1e-05
MASKED = -1000000000.0
F32 = jnp.float32
BF16 = jnp.bfloat16
VMEM = pltpu.VMEM
SMEM = pltpu.SMEM


def mm(a, b):
    return lax.dot_general(a, b, (((1,), (0,)), ((), ())), preferred_element_type=F32)


def mm_nt(a, b):
    return lax.dot_general(a, b, (((1,), (1,)), ((), ())), preferred_element_type=F32)


def mm_tn(a, b):
    return lax.dot_general(a, b, (((0,), (0,)), ((), ())), preferred_element_type=F32)


def normalise(values, gain):
    average = jnp.mean(values, axis=-1, keepdims=True)
    centred = values - average
    spread = jnp.mean(centred * centred, axis=-1, keepdims=True)
    return (centred * lax.rsqrt(spread + EPSILON) * gain).astype(BF16)


def sigmoid(values):
    return 1.0 / (1.0 + jnp.exp(-values))


def membership(tok, count, tokens):
    atoms = tok.shape[1]
    slot = lax.broadcasted_iota(jnp.int32, (tokens, atoms), 1)
    name = lax.broadcasted_iota(jnp.int32, (tokens, atoms), 0)
    return (tok == name) & (slot < count)


def atom_body(
    info, x, before, after, tok, bias, gain, qkvg, proj, lift, tsingle, tgain,
    normed_out, hidden_out, mid_out, en, pj, att,
):
    count, low, high = info[0], info[1], info[2]
    atoms = x.shape[0]
    tokens = tsingle.shape[0]
    rows = LEFT_RIM + atoms + RIGHT_RIM
    en[0:LEFT_RIM, :] = normalise(before[...].astype(F32), gain[...])
    en[LEFT_RIM : LEFT_RIM + atoms, :] = normalise(x[...].astype(F32), gain[...])
    en[LEFT_RIM + atoms :, :] = jnp.zeros((RIGHT_RIM, AW), BF16)
    late = normalise(after[...].astype(F32), gain[...])
    place = lax.broadcasted_iota(jnp.int32, (rows, RIGHT_RIM), 0) - (LEFT_RIM + count)
    pick = place == lax.broadcasted_iota(jnp.int32, (rows, RIGHT_RIM), 1)
    moved = mm(jnp.where(pick, 1.0, 0.0).astype(BF16), late)
    line = lax.broadcasted_iota(jnp.int32, (rows, AW), 0) - (LEFT_RIM + count)
    inside = (line >= 0) & (line < RIGHT_RIM)
    normed = jnp.where(inside, moved, en[...].astype(F32)).astype(BF16)
    pj[...] = mm(normed, qkvg[...]).astype(BF16)
    lane = lax.broadcasted_iota(jnp.int32, (WQ, AW), 1) // AD
    spot = lax.broadcasted_iota(jnp.int32, (1, WK), 1)
    for w in range(atoms // WQ):
        q = pj[LEFT_RIM + WQ * w : LEFT_RIM + WQ * (w + 1), 0:AW]
        k = pj[WQ * w : WQ * w + WK, AW : 2 * AW]
        v = pj[WQ * w : WQ * w + WK, 2 * AW : 3 * AW]
        spread_q = jnp.concatenate(
            [jnp.where(lane == h, q, jnp.zeros_like(q)) for h in range(AH)], axis=0
        )
        scores = mm_nt(spread_q, k) * AD ** (-0.5)
        scores = scores + bias[w].reshape(AH * WQ, WK).astype(F32)
        p = spot + (WQ * w - LEFT_RIM)
        scores = jnp.where((p >= low) & (p < high), scores, MASKED)
        raised = jnp.exp(scores - jnp.max(scores, axis=-1, keepdims=True))
        total = jnp.sum(raised, axis=-1, keepdims=True)
        mixed = mm(raised.astype(BF16), v) * (1.0 / total)
        out = jnp.zeros((WQ, AW), F32)
        for h in range(AH):
            out = jnp.where(lane == h, mixed[WQ * h : WQ * (h + 1)], out)
        att[WQ * w : WQ * (w + 1), :] = out
    gate = pj[LEFT_RIM : LEFT_RIM + atoms, 3 * AW :].astype(F32)
    gated = (att[...] * sigmoid(gate)).astype(BF16)
    mid = (x[...].astype(F32) + mm(gated, proj[...])).astype(BF16)
    mid_out[...] = mid
    lifted = jnp.maximum(mm(mid, lift[...]), 0.0).astype(BF16)
    member = jnp.where(membership(tok[...], count, tokens), 1.0, 0.0)
    summed = mm(member.astype(BF16), lifted)
    counts = jnp.sum(member, axis=1, keepdims=True)
    hidden = tsingle[...].astype(F32) + summed / counts
    hidden_out[...] = hidden
    normed_out[...] = normalise(hidden, tgain[...])


def head_windows():
    windows = []
    h = 0
    while h < TH:
        first = h * TD // 128 * 128
        first = min(first, TW - 256)
        heads = []
        while h < TH and (h + 1) * TD <= first + 256:
            heads.append(h)
            h += 1
        windows.append((first, heads))
    return windows


def token_body(nchip, *refs):
    own, oth = refs[1 : 1 + nchip], refs[1 + nchip : 1 + 2 * nchip]
    info = refs[0]
    (normed, hidden_in, mid, tok, bias, qg, kv, proj, down,
     atom_out, token_out, xs, kvs, qs, st, acc) = refs[1 + 2 * nchip :]
    count, chip, core = info[0], info[3], info[4]
    tokens = normed.shape[0]
    pair = 2 * tokens
    atoms = mid.shape[0]
    query_gate = mm(normed[...], qg[...]).astype(BF16)
    windows = head_windows()
    column = lax.broadcasted_iota(jnp.int32, (tokens, 256), 1)
    for first, heads in windows:
        q = query_gate[:, first : first + 256]
        for h in heads:
            keep = (column >= h * TD - first) & (column < (h + 1) * TD - first)
            qs[h * tokens : (h + 1) * tokens, :] = jnp.where(keep, q, jnp.zeros_like(q))
    for j in range(nchip):
        xs[pl.ds(pl.multiple_of(j * pair + core * tokens, tokens), tokens), :] = own[j][...]
        xs[pl.ds(pl.multiple_of(j * pair + (1 - core) * tokens, tokens), tokens), :] = oth[j][...]
    group = min(nchip, 4)
    keys = group * pair
    for g in range(nchip // group):
        kvs[...] = mm(xs[g * keys : (g + 1) * keys, :], kv[...]).astype(BF16)
        for first, heads in windows:
            rows = slice(heads[0] * tokens, (heads[-1] + 1) * tokens)
            scores = mm_nt(qs[rows, :], kvs[:, first : first + 256]) * TD ** (-0.5)
            parts = []
            for j in range(group):
                at = pl.multiple_of((chip ^ (g * group + j)) * pair, pair)
                tile = bias[heads[0] : heads[-1] + 1, :, pl.ds(at, pair)]
                parts.append(
                    scores[:, j * pair : (j + 1) * pair]
                    + tile.reshape(len(heads) * tokens, pair).astype(F32)
                )
            best = parts[0]
            for part in parts[1:]:
                best = jnp.maximum(best, part)
            best = jnp.max(best, axis=-1, keepdims=True)
            if g:
                old = st[rows, 0:1]
                best = jnp.maximum(best, old)
            raised = [jnp.exp(part - best) for part in parts]
            total = raised[0]
            for part in raised[1:]:
                total = total + part
            total = jnp.sum(total, axis=-1, keepdims=True)
            weights = jnp.concatenate([part.astype(BF16) for part in raised], axis=1)
            mixed = mm(weights, kvs[:, TW + first : TW + first + 256])
            if g:
                factor = jnp.exp(old - best)
                total = total + factor * st[rows, 1:2]
                mixed = mixed + factor * acc[rows, :]
            if g + 1 < nchip // group:
                st[rows, 0:1] = best
                st[rows, 1:2] = total
                acc[rows, :] = mixed
            else:
                acc[rows, :] = mixed * (1.0 / total)
    pieces = [jnp.zeros((tokens, 128), F32) for _ in range(TW // 128)]
    tile_column = lax.broadcasted_iota(jnp.int32, (tokens, 128), 1)
    for first, heads in windows:
        for h in heads:
            for half in range(2):
                t = first // 128 + half
                a, b = h * TD - t * 128, (h + 1) * TD - t * 128
                if b <= 0 or a >= 128:
                    continue
                keep = (tile_column >= a) & (tile_column < b)
                value = acc[h * tokens : (h + 1) * tokens, half * 128 : (half + 1) * 128]
                pieces[t] = jnp.where(keep, value, pieces[t])
    attended = jnp.concatenate(pieces, axis=1)
    gated = (attended * sigmoid(query_gate[:, TW:].astype(F32))).astype(BF16)
    final = (hidden_in[...] + mm(gated, proj[...])).astype(BF16)
    token_out[...] = final
    back = mm(final, down[...])
    member = jnp.where(membership(tok[...], count, tokens), 1.0, 0.0).astype(BF16)
    high = back.astype(BF16)
    rest = back - high.astype(F32)
    low = rest.astype(BF16)
    lowest = (rest - low.astype(F32)).astype(BF16)
    spread = mm_tn(member, high) + (mm_tn(member, low) + mm_tn(member, lowest))
    live = lax.broadcasted_iota(jnp.int32, (atoms, AW), 0) < count
    atom_out[...] = jnp.where(live, mid[...].astype(F32) + spread, 0.0).astype(BF16)


def whole_spec(count):
    return [pl.BlockSpec(memory_space=VMEM) for _ in range(count)]


def solution(mesh):
    width = mesh.shape["row"]
    nchip = width // 2

    def swap(value, bits):
        return lax.ppermute(value, "row", [(i, i ^ bits) for i in range(width)])

    def on_device(
        atom_single, atom_count, atom_token, atom_bias, token_single, token_bias, atom_gain,
        atom_qkvg, atom_proj, atom_to_token, token_gain, token_qg, token_kv, token_proj,
        token_to_atom,
    ):
        atoms = atom_single.shape[0]
        tokens = token_single.shape[0]
        row = lax.axis_index("row")
        count = atom_count[row]
        tail = lax.dynamic_slice_in_dim(atom_single, count - LEFT_RIM, LEFT_RIM, 0)
        before = lax.ppermute(tail, "row", [(i, i + 1) for i in range(width - 1)])
        after = lax.ppermute(
            atom_single[:RIGHT_RIM], "row", [(i + 1, i) for i in range(width - 1)]
        )
        far = 4 * atoms
        low = jnp.where(row == 0, 0, -far)
        high = jnp.where(row == width - 1, count, far)
        info = jnp.stack([count, low, high, row // 2, row % 2]).astype(jnp.int32)
        tok = atom_token.reshape(1, atoms)
        rows = LEFT_RIM + atoms + RIGHT_RIM
        normed, hidden, mid = pl.pallas_call(
            atom_body,
            out_shape=(
                jax.ShapeDtypeStruct((tokens, TW), BF16),
                jax.ShapeDtypeStruct((tokens, TW), F32),
                jax.ShapeDtypeStruct((atoms, AW), BF16),
            ),
            in_specs=[pl.BlockSpec(memory_space=SMEM)] + whole_spec(11),
            out_specs=tuple(whole_spec(3)),
            scratch_shapes=[
                VMEM((rows, AW), BF16), VMEM((rows, 4 * AW), BF16), VMEM((atoms, AW), F32),
            ],
            name="atoms",
        )(
            info, atom_single, before, after, tok, atom_bias, atom_gain.reshape(1, AW),
            atom_qkvg, atom_proj, atom_to_token, token_single, token_gain.reshape(1, TW),
        )
        blocks = {0: normed}
        for k in range(1, nchip):
            top = 1 << (k.bit_length() - 1)
            blocks[k] = swap(blocks[k ^ top] if k == top else blocks[top], 2 * (top if k == top else k ^ top))
        own = [blocks[k] for k in range(nchip)]
        oth = [swap(b, 1) for b in own]
        keys = min(nchip, 4) * 2 * tokens
        atom_out, token_out = pl.pallas_call(
            lambda *refs: token_body(nchip, *refs),
            out_shape=(
                jax.ShapeDtypeStruct((atoms, AW), BF16),
                jax.ShapeDtypeStruct((tokens, TW), BF16),
            ),
            in_specs=[pl.BlockSpec(memory_space=SMEM)] + whole_spec(2 * nchip + 9),
            out_specs=tuple(whole_spec(2)),
            scratch_shapes=[
                VMEM((width * tokens, TW), BF16),
                VMEM((keys, 2 * TW), BF16),
                VMEM((TH * tokens, 256), BF16),
                VMEM((TH * tokens, 128), F32),
                VMEM((TH * tokens, 256), F32),
            ],
            name="tokens",
        )(
            info, *own, *oth, normed, hidden, mid, tok, token_bias, token_qg, token_kv,
            token_proj, token_to_atom,
        )
        return atom_out, token_out

    split = P(("sample", "row"), None)
    return jax.shard_map(
        on_device,
        mesh=mesh,
        in_specs=(
            split, P(), P("row"), P("row", None, None, None), split, P(None, "row", None),
            P(), P(), P(), P(), P(), P(), P(), P(), P(),
        ),
        out_specs=(split, split),
        check_vma=False,
    )
```

```python
import jax
import jax.numpy as jnp
from jax import lax
from jax.experimental import pallas as pl
from jax.experimental.pallas import tpu as pltpu
from jax.sharding import PartitionSpec as P


TW = 768
TH = 16
AW = 128
AH = 4
WQ = 32
WK = 128
LEFT_RIM = 48
RIGHT_RIM = 80
AD = AW // AH
TD = TW // TH

EPSILON = 1e-05
MASKED = -1000000000.0
F32 = jnp.float32
BF16 = jnp.bfloat16
VMEM = pltpu.VMEM
SMEM = pltpu.SMEM


def mm(a, b):
    return lax.dot_general(a, b, (((1,), (0,)), ((), ())), preferred_element_type=F32)


def mm_nt(a, b):
    return lax.dot_general(a, b, (((1,), (1,)), ((), ())), preferred_element_type=F32)


def mm_tn(a, b):
    return lax.dot_general(a, b, (((0,), (0,)), ((), ())), preferred_element_type=F32)


def normalise(values, gain):
    average = jnp.mean(values, axis=-1, keepdims=True)
    centred = values - average
    spread = jnp.mean(centred * centred, axis=-1, keepdims=True)
    return (centred * lax.rsqrt(spread + EPSILON) * gain).astype(BF16)


def sigmoid(values):
    return 1.0 / (1.0 + jnp.exp(-values))


def membership(tok, count, tokens):
    atoms = tok.shape[1]
    slot = lax.broadcasted_iota(jnp.int32, (tokens, atoms), 1)
    name = lax.broadcasted_iota(jnp.int32, (tokens, atoms), 0)
    return (tok == name) & (slot < count)


def attend_window(q, k, v, bias, first, low, high):
    lane = lax.broadcasted_iota(jnp.int32, (WQ, AW), 1) // AD
    spread_q = jnp.concatenate(
        [jnp.where(lane == h, q, jnp.zeros_like(q)) for h in range(AH)], axis=0
    )
    scores = mm_nt(spread_q, k) * AD ** (-0.5)
    scores = scores + bias.reshape(AH * WQ, WK).astype(F32)
    p = lax.broadcasted_iota(jnp.int32, (1, WK), 1) + first
    scores = jnp.where((p >= low) & (p < high), scores, MASKED)
    raised = jnp.exp(scores - jnp.max(scores, axis=-1, keepdims=True))
    both = mm(raised.astype(BF16), jnp.concatenate([v, jnp.ones_like(v)], axis=1))
    mixed = both[:, :AW] / both[:, AW:]
    out = jnp.zeros((WQ, AW), F32)
    for h in range(AH):
        out = jnp.where(lane == h, mixed[WQ * h : WQ * (h + 1)], out)
    return out


def early_body(
    info, x_hbm, bias_hbm, gain, qkvg_hbm, q_out, kv_out, gate_out, att_out, x, bias, qkvg, sems
):
    row = lax.axis_index("row")
    count = info[row]
    atoms = x.shape[0]
    half = atoms // WQ // 2
    copies = [
        pltpu.make_async_copy(x_hbm, x, sems.at[0]),
        pltpu.make_async_copy(qkvg_hbm, qkvg, sems.at[1]),
        pltpu.make_async_copy(bias_hbm.at[:half], bias.at[:half], sems.at[2]),
        pltpu.make_async_copy(bias_hbm.at[half:], bias.at[half:], sems.at[3]),
    ]
    for copy in copies:
        copy.start()
    copies[0].wait()
    normed = normalise(x[...].astype(F32), gain[...])
    copies[1].wait()
    parts = mm(normed, qkvg[...]).astype(BF16)
    q_out[...] = parts[:, :AW]
    gate_out[...] = parts[:, 3 * AW :]
    kv_out[0:LEFT_RIM, :] = jnp.zeros((LEFT_RIM, 2 * AW), BF16)
    kv_out[LEFT_RIM : LEFT_RIM + atoms, :] = parts[:, AW : 3 * AW]
    kv_out[LEFT_RIM + atoms :, :] = jnp.zeros((RIGHT_RIM, 2 * AW), BF16)
    for w in range(atoms // WQ):
        if w % half == 0:
            copies[2 + w // half].wait()
        rows = slice(WQ * w, WQ * w + WK)
        att_out[WQ * w : WQ * (w + 1), :] = attend_window(
            q_out[WQ * w : WQ * (w + 1), :], kv_out[rows, :AW], kv_out[rows, AW:],
            bias[w], WQ * w - LEFT_RIM, 0, count,
        )


def late_body(
    info, near, far, q, kv_in, gate_in, att_in, tok, gain, tgain, bias, qkvg_hbm, x_hbm, proj_hbm,
    lift_hbm, tsingle_hbm, normed_out, hidden_out, mid_out, kv, att, some, qkvg, x, proj, lift,
    tsingle, sems,
):
    row = lax.axis_index("row")
    width = lax.axis_size("row")
    count = info[row]
    atoms = x.shape[0]
    tokens = tsingle.shape[0]
    last = (count - 1) // WQ
    head = pltpu.make_async_copy(bias.at[0:2], some.at[0:2], sems.at[0])
    head.start()
    tail = pltpu.make_async_copy(bias.at[pl.ds(last - 2, 3)], some.at[2:5], sems.at[1])
    tail.start()
    copies = [
        pltpu.make_async_copy(source, target, sems.at[2 + i])
        for i, (source, target) in enumerate(
            [
                (qkvg_hbm.at[:, AW : 3 * AW], qkvg), (x_hbm, x), (proj_hbm, proj),
                (lift_hbm, lift), (tsingle_hbm, tsingle),
            ]
        )
    ]
    for copy in copies:
        copy.start()
    odd = row % 2 == 1
    previous = jnp.where(odd, near[...], far[...])
    following = jnp.where(odd, far[0:RIGHT_RIM, :], near[0:RIGHT_RIM, :])
    before_count = info[jnp.maximum(row - 1, 0)]
    r = lax.broadcasted_iota(jnp.int32, (LEFT_RIM, atoms), 0) + (before_count - LEFT_RIM)
    pick = r == lax.broadcasted_iota(jnp.int32, (LEFT_RIM, atoms), 1)
    before = mm(jnp.where(pick, 1.0, 0.0).astype(BF16), previous)
    rims = jnp.concatenate([before, following.astype(F32)], axis=0)
    rims = normalise(rims, gain[...])
    copies[0].wait()
    rim_kv = mm(rims, qkvg[...]).astype(BF16)
    after_kv = rim_kv[LEFT_RIM:]
    kv[...] = kv_in[...]
    kv[0:LEFT_RIM, :] = rim_kv[:LEFT_RIM]
    att[...] = att_in[...]
    low = jnp.where(row == 0, 0, -4 * atoms)
    high = jnp.where(row == width - 1, count, 4 * atoms)
    region = 2 * WQ + WK
    start = pl.multiple_of((last - 2) * WQ, WQ)
    r = lax.broadcasted_iota(jnp.int32, (region, RIGHT_RIM), 0) + (start - LEFT_RIM - count)
    pick = r == lax.broadcasted_iota(jnp.int32, (region, RIGHT_RIM), 1)
    moved = mm(jnp.where(pick, 1.0, 0.0).astype(BF16), after_kv)
    r = lax.broadcasted_iota(jnp.int32, (region, 2 * AW), 0) + (start - LEFT_RIM - count)
    local = kv[pl.ds(start, region), :].astype(F32)
    local = jnp.where((r >= 0) & (r < RIGHT_RIM), moved, local).astype(BF16)
    head.wait()
    tail.wait()
    for w in range(2):
        rows = slice(WQ * w, WQ * w + WK)
        att[WQ * w : WQ * (w + 1), :] = attend_window(
            q[WQ * w : WQ * (w + 1), :], kv[rows, :AW], kv[rows, AW:], some[w],
            WQ * w - LEFT_RIM, low, high,
        )
    for w in range(3):
        at = pl.multiple_of(start + WQ * w, WQ)
        rows = slice(WQ * w, WQ * w + WK)
        att[pl.ds(at, WQ), :] = attend_window(
            q[pl.ds(at, WQ), :], local[rows, :AW], local[rows, AW:], some[2 + w],
            at - LEFT_RIM, low, high,
        )
    gated = (att[...] * sigmoid(gate_in[...].astype(F32))).astype(BF16)
    copies[1].wait()
    copies[2].wait()
    mid = (x[...].astype(F32) + mm(gated, proj[...])).astype(BF16)
    mid_out[...] = mid
    copies[3].wait()
    lifted = jnp.maximum(mm(mid, lift[...]), 0.0).astype(BF16)
    member = jnp.where(membership(tok[...], count, tokens), 1.0, 0.0)
    summed = mm(member.astype(BF16), lifted)
    counts = jnp.sum(member, axis=1, keepdims=True)
    copies[4].wait()
    hidden = tsingle[...].astype(F32) + summed / counts
    hidden_out[...] = hidden
    normed_out[...] = normalise(hidden, tgain[...])


def head_windows():
    windows = []
    h = 0
    while h < TH:
        first = h * TD // 128 * 128
        first = min(first, TW - 256)
        heads = []
        while h < TH and (h + 1) * TD <= first + 256:
            heads.append(h)
            h += 1
        windows.append((first, heads))
    return windows


def query_body(info, normed, tok, qg, out, member_out, normed_out):
    tokens = normed.shape[0]
    member = membership(tok[...], info[lax.axis_index("row")], tokens)
    r = lax.broadcasted_iota(jnp.int32, (tokens, 3 * tokens), 0)
    c = lax.broadcasted_iota(jnp.int32, (tokens, 3 * tokens), 1)
    same = (c == r) | (c == r + tokens) | (c == r + 2 * tokens)
    one = jnp.where(member, 1.0, 0.0).astype(BF16)
    member_out[...] = mm_tn(one, jnp.where(same, 1.0, 0.0).astype(BF16)).astype(BF16)
    normed_out[...] = normed[...]
    out[...] = mm(normed[...], qg[...]).astype(BF16)


def token_body(offsets, begins, ends, *refs):
    number = len(offsets)
    own, oth, refs = refs[:number], refs[number : 2 * number], refs[2 * number :]
    query_gate, kv, bias, *refs = refs
    if not begins:
        st_in, acc_in, *refs = refs
    if ends:
        info, hidden_in, mid, member, proj_hbm, down, atom_out, token_out, *refs = refs
        xs, kvs, qs, proj, sems = refs
    else:
        st_out, acc_out, *refs = refs
        xs, kvs, qs = refs
    row = lax.axis_index("row")
    chip, core = row // 2, row % 2
    tokens = own[0].shape[0]
    pair = 2 * tokens
    keys = number * pair
    if ends:
        fetch = pltpu.make_async_copy(proj_hbm, proj, sems.at[0])
        fetch.start()
    for j in range(number):
        at = pl.multiple_of(j * pair + core * tokens, tokens)
        xs[pl.ds(at, tokens), :] = own[j][...]
        at = pl.multiple_of(j * pair + (1 - core) * tokens, tokens)
        xs[pl.ds(at, tokens), :] = oth[j][...]
    column = lax.broadcasted_iota(jnp.int32, (tokens, 256), 1)
    windows = head_windows()
    for first, heads in windows:
        q = query_gate[:, first : first + 256]
        for h in heads:
            keep = (column >= h * TD - first) & (column < (h + 1) * TD - first)
            qs[h * tokens : (h + 1) * tokens, :] = jnp.where(keep, q, jnp.zeros_like(q))
    kvs[...] = mm(xs[...], kv[...]).astype(BF16)
    places = [pl.multiple_of((chip ^ offset) * pair, pair) for offset in offsets]
    pieces = [jnp.zeros((tokens, 128), F32) for _ in range(TW // 128)]
    tile_column = lax.broadcasted_iota(jnp.int32, (tokens, 128), 1)
    key_column = lax.broadcasted_iota(jnp.int32, (keys, 256), 1)
    for first, heads in windows:
        rows = slice(heads[0] * tokens, (heads[-1] + 1) * tokens)
        used = (heads[0] * TD - first, (heads[-1] + 1) * TD - first)
        spare = 255 if used[1] < 256 else 0
        scores = mm_nt(qs[rows, :], kvs[:, first : first + 256]) * TD ** (-0.5)
        tile = jnp.concatenate(
            [
                bias[heads[0] : heads[-1] + 1, :, pl.ds(at, pair)].reshape(-1, pair)
                for at in places
            ],
            axis=1,
        )
        scores = scores + tile.astype(F32)
        best = jnp.broadcast_to(jnp.max(scores, axis=-1, keepdims=True), (scores.shape[0], 128))
        if not begins:
            best = jnp.maximum(best, st_in[rows, :])
        raised = jnp.concatenate(
            [
                jnp.exp(scores[:, i : i + 128] - best).astype(BF16)
                for i in range(0, keys, 128)
            ],
            axis=1,
        )
        values = kvs[:, TW + first : TW + first + 256]
        values = jnp.where(
            (key_column >= used[0]) & (key_column < used[1]), values, jnp.ones_like(values)
        )
        mixed = mm(raised, values)
        if not begins:
            factor = jnp.exp(st_in[rows, :] - best)
            mixed = mixed + jnp.concatenate([factor, factor], axis=1) * acc_in[rows, :]
        if not ends:
            st_out[rows, :] = best
            acc_out[rows, :] = mixed
            continue
        inverse = 1.0 / mixed[:, spare : spare + 1]
        for i, h in enumerate(heads):
            part = slice(i * tokens, (i + 1) * tokens)
            for half in range(2):
                t = first // 128 + half
                a, b = h * TD - t * 128, (h + 1) * TD - t * 128
                if b <= 0 or a >= 128:
                    continue
                keep = (tile_column >= a) & (tile_column < b)
                value = mixed[part, half * 128 : (half + 1) * 128] * inverse[part]
                pieces[t] = jnp.where(keep, value, pieces[t])
    if not ends:
        return
    attended = jnp.concatenate(pieces, axis=1)
    count = info[row]
    atoms = mid.shape[0]
    gated = (attended * sigmoid(query_gate[:, TW:].astype(F32))).astype(BF16)
    fetch.wait()
    final = (hidden_in[...] + mm(gated, proj[...])).astype(BF16)
    token_out[...] = final
    back = mm(final, down[...])
    high = back.astype(BF16)
    rest = back - high.astype(F32)
    low = rest.astype(BF16)
    lowest = (rest - low.astype(F32)).astype(BF16)
    spread = mm(member[...], jnp.concatenate([high, low, lowest], axis=0))
    live = lax.broadcasted_iota(jnp.int32, (atoms, AW), 0) < count
    atom_out[...] = jnp.where(live, mid[...].astype(F32) + spread, 0.0).astype(BF16)


def vmem(count):
    return [pl.BlockSpec(memory_space=VMEM) for _ in range(count)]


def anywhere(count):
    return [pl.BlockSpec(memory_space=pltpu.HBM) for _ in range(count)]


def scalars():
    return [pl.BlockSpec(memory_space=SMEM)]


def like(shape, dtype):
    return jax.ShapeDtypeStruct(shape, dtype)


def solution(mesh):
    width = mesh.shape["row"]
    nchip = width // 2
    groups = [list(range(k, min(k + 4, nchip))) for k in range(0, nchip, 4)]
    if nchip == 8:
        groups = [[0, 1, 2, 4], [3, 5, 6, 7]]

    def swap(value, bits):
        return lax.ppermute(value, "row", [(i, i ^ bits) for i in range(width)])

    def on_device(
        atom_single, atom_count, atom_token, atom_bias, token_single, token_bias, atom_gain,
        atom_qkvg, atom_proj, atom_to_token, token_gain, token_qg, token_kv, token_proj,
        token_to_atom,
    ):
        atoms = atom_single.shape[0]
        tokens = token_single.shape[0]
        rows = LEFT_RIM + atoms + RIGHT_RIM
        far = lax.ppermute(
            atom_single, "row",
            [(i, i + 1 if i % 2 else i - 1) for i in range(1, width - 1)],
        )
        near = swap(atom_single, 1)
        tok = atom_token.reshape(1, atoms)
        gain = atom_gain.reshape(1, AW)
        q, kv, gate, att = pl.pallas_call(
            early_body,
            out_shape=(
                like((atoms, AW), BF16), like((rows, 2 * AW), BF16), like((atoms, AW), BF16),
                like((atoms, AW), F32),
            ),
            in_specs=scalars() + anywhere(2) + vmem(1) + anywhere(1),
            out_specs=tuple(vmem(4)),
            scratch_shapes=[
                VMEM((atoms, AW), BF16), VMEM(atom_bias.shape, BF16), VMEM((AW, 4 * AW), BF16),
                pltpu.SemaphoreType.DMA((4,)),
            ],
            cost_estimate=pl.CostEstimate(
                flops=2 * atoms * AW * (4 * AW + 3 * WK * AH), transcendentals=atoms * AH * WK,
                bytes_accessed=8 << 20,
            ),
            name="early",
        )(atom_count, atom_single, atom_bias, gain, atom_qkvg)
        normed, hidden, mid = pl.pallas_call(
            late_body,
            out_shape=(like((tokens, TW), BF16), like((tokens, TW), F32), like((atoms, AW), BF16)),
            in_specs=scalars() + vmem(9) + anywhere(6),
            out_specs=tuple(vmem(3)),
            scratch_shapes=[
                VMEM((rows, 2 * AW), BF16), VMEM((atoms, AW), F32),
                VMEM((5, AH, WQ, WK), BF16), VMEM((AW, 2 * AW), BF16), VMEM((atoms, AW), BF16),
                VMEM((AW, AW), BF16), VMEM((AW, TW), BF16), VMEM((tokens, TW), BF16),
                pltpu.SemaphoreType.DMA((7,)),
            ],
            compiler_params=pltpu.CompilerParams(vmem_limit_bytes=59200 << 10),
            cost_estimate=pl.CostEstimate(
                flops=4 * atoms * AW * TW, transcendentals=atoms * AH * WK, bytes_accessed=8 << 20,
            ),
            name="late",
        )(
            atom_count, near, far, q, kv, gate, att, tok, gain, token_gain, atom_bias,
            atom_qkvg, atom_single, atom_proj, atom_to_token, token_single,
        )
        blocks, other = {0: normed}, {}
        for k in range(1, nchip):
            top = 1 << (k.bit_length() - 1)
            blocks[k] = swap(normed if k == top else blocks[top], 2 * (k if k == top else k ^ top))
        for k in range(nchip):
            other[k] = swap(blocks[k], 1)
        query_gate, member, normed_again = pl.pallas_call(
            query_body,
            out_shape=(
                like((tokens, 2 * TW), BF16), like((atoms, 3 * tokens), BF16),
                like((tokens, TW), BF16),
            ),
            in_specs=scalars() + vmem(3),
            out_specs=tuple(vmem(3)),
            compiler_params=pltpu.CompilerParams(vmem_limit_bytes=8 << 20),
            name="queries",
        )(atom_count, normed, tok, token_qg)
        blocks[0] = normed_again
        state = ()
        for offsets in groups:
            begin = offsets[0]
            begins, ends = begin == 0, offsets[-1] == nchip - 1
            number = len(offsets)
            keys = number * 2 * tokens
            arrays = [blocks[k] for k in offsets] + [other[k] for k in offsets]
            arrays += [query_gate, token_kv, token_bias, *state]
            specs = vmem(2 * number + 3 + len(state))
            scratch = [
                VMEM((keys, TW), BF16), VMEM((keys, 2 * TW), BF16), VMEM((TH * tokens, 256), BF16),
            ]
            if ends:
                arrays += [atom_count, hidden, mid, member, token_proj, token_to_atom]
                specs += scalars() + vmem(3) + anywhere(1) + vmem(1)
                outs = (like((atoms, AW), BF16), like((tokens, TW), BF16))
                scratch += [VMEM((TW, TW), BF16), pltpu.SemaphoreType.DMA((1,))]
            else:
                outs = (like((TH * tokens, 128), F32), like((TH * tokens, 256), F32))
            state = pl.pallas_call(
                lambda *refs: token_body(offsets, begins, ends, *refs),
                out_shape=outs,
                in_specs=specs,
                out_specs=tuple(vmem(2)),
                scratch_shapes=scratch,
                compiler_params=pltpu.CompilerParams(vmem_limit_bytes=16 << 20),
            )(*arrays)
        return state

    split = P(("sample", "row"), None)
    return jax.shard_map(
        on_device,
        mesh=mesh,
        in_specs=(
            split, P(), P("row"), P("row", None, None, None), split, P(None, "row", None),
            P(), P(), P(), P(), P(), P(), P(), P(), P(),
        ),
        out_specs=(split, split),
        check_vma=False,
    )
```

```python
import jax
import jax.numpy as jnp
from jax import lax
from jax.experimental import pallas as pl
from jax.experimental.pallas import tpu as pltpu
from jax.sharding import PartitionSpec as P


TW = 768
TH = 16
AW = 128
AH = 4
WQ = 32
WK = 128
LEFT_RIM = 48
RIGHT_RIM = 80
AD = AW // AH
TD = TW // TH

EPSILON = 1e-05
MASKED = -1000000000.0
F32 = jnp.float32
BF16 = jnp.bfloat16
VMEM = pltpu.VMEM
SMEM = pltpu.SMEM


def mm(a, b):
    return lax.dot_general(a, b, (((1,), (0,)), ((), ())), preferred_element_type=F32)


def mm_nt(a, b):
    return lax.dot_general(a, b, (((1,), (1,)), ((), ())), preferred_element_type=F32)


def mm_tn(a, b):
    return lax.dot_general(a, b, (((0,), (0,)), ((), ())), preferred_element_type=F32)


def normalise(values, gain):
    average = jnp.mean(values, axis=-1, keepdims=True)
    centred = values - average
    spread = jnp.mean(centred * centred, axis=-1, keepdims=True)
    return (centred * lax.rsqrt(spread + EPSILON) * gain).astype(BF16)


def sigmoid(values):
    return 1.0 / (1.0 + jnp.exp(-values))


def membership(tok, count, tokens):
    atoms = tok.shape[1]
    slot = lax.broadcasted_iota(jnp.int32, (tokens, atoms), 1)
    name = lax.broadcasted_iota(jnp.int32, (tokens, atoms), 0)
    return (tok == name) & (slot < count)


def attend_window(q, k, v, bias, first, low, high):
    lane = lax.broadcasted_iota(jnp.int32, (WQ, AW), 1) // AD
    spread_q = jnp.concatenate(
        [jnp.where(lane == h, q, jnp.zeros_like(q)) for h in range(AH)], axis=0
    )
    scores = mm_nt(spread_q, k) * AD ** (-0.5)
    scores = scores + bias.reshape(AH * WQ, WK).astype(F32)
    p = lax.broadcasted_iota(jnp.int32, (1, WK), 1) + first
    scores = jnp.where((p >= low) & (p < high), scores, MASKED)
    raised = jnp.exp(scores - jnp.max(scores, axis=-1, keepdims=True))
    both = mm(raised.astype(BF16), jnp.concatenate([v, jnp.ones_like(v)], axis=1))
    mixed = both[:, :AW] / both[:, AW:]
    out = jnp.zeros((WQ, AW), F32)
    for h in range(AH):
        out = jnp.where(lane == h, mixed[WQ * h : WQ * (h + 1)], out)
    return out


def early_body(info, x, bias, gain, qkvg, q_out, kv_out, gate_out, gated_out):
    row = lax.axis_index("row")
    count = info[row]
    atoms = x.shape[0]
    normed = normalise(x[...].astype(F32), gain[...])
    parts = mm(normed, qkvg[...]).astype(BF16)
    q_out[...] = parts[:, :AW]
    gate_out[...] = parts[:, 3 * AW :]
    kv_out[0:LEFT_RIM, :] = jnp.zeros((LEFT_RIM, 2 * AW), BF16)
    kv_out[LEFT_RIM : LEFT_RIM + atoms, :] = parts[:, AW : 3 * AW]
    kv_out[LEFT_RIM + atoms :, :] = jnp.zeros((RIGHT_RIM, 2 * AW), BF16)
    for w in range(atoms // WQ):
        rows = slice(WQ * w, WQ * w + WK)
        own = slice(WQ * w, WQ * (w + 1))
        out = attend_window(
            q_out[own, :], kv_out[rows, :AW], kv_out[rows, AW:],
            bias[w], WQ * w - LEFT_RIM, 0, count,
        )
        gated_out[own, :] = (out * sigmoid(gate_out[own, :].astype(F32))).astype(BF16)


def late_body(
    info, near, far, q, kv_in, gate_in, gated_in, tok, gain, tgain, bias, qkvg, x, proj, lift,
    tsingle, normed_out, hidden_out, mid_out, kv, gated,
):
    row = lax.axis_index("row")
    width = lax.axis_size("row")
    count = info[row]
    atoms = x.shape[0]
    tokens = tsingle.shape[0]
    last = (count - 1) // WQ
    odd = row % 2 == 1
    previous = jnp.where(odd, near[...], far[...])
    following = jnp.where(odd, far[0:RIGHT_RIM, :], near[0:RIGHT_RIM, :])
    before_count = info[jnp.maximum(row - 1, 0)]
    r = lax.broadcasted_iota(jnp.int32, (LEFT_RIM, atoms), 0) + (before_count - LEFT_RIM)
    pick = r == lax.broadcasted_iota(jnp.int32, (LEFT_RIM, atoms), 1)
    before = mm(jnp.where(pick, 1.0, 0.0).astype(BF16), previous)
    rims = jnp.concatenate([before, following.astype(F32)], axis=0)
    rim_kv = mm(normalise(rims, gain[...]), qkvg[:, AW : 3 * AW]).astype(BF16)
    after_kv = rim_kv[LEFT_RIM:]
    kv[...] = kv_in[...]
    kv[0:LEFT_RIM, :] = rim_kv[:LEFT_RIM]
    gated[...] = gated_in[...]
    low = jnp.where(row == 0, 0, -4 * atoms)
    high = jnp.where(row == width - 1, count, 4 * atoms)
    region = 2 * WQ + WK
    start = pl.multiple_of((last - 2) * WQ, WQ)
    r = lax.broadcasted_iota(jnp.int32, (region, RIGHT_RIM), 0) + (start - LEFT_RIM - count)
    pick = r == lax.broadcasted_iota(jnp.int32, (region, RIGHT_RIM), 1)
    moved = mm(jnp.where(pick, 1.0, 0.0).astype(BF16), after_kv)
    r = lax.broadcasted_iota(jnp.int32, (region, 2 * AW), 0) + (start - LEFT_RIM - count)
    local = kv[pl.ds(start, region), :].astype(F32)
    local = jnp.where((r >= 0) & (r < RIGHT_RIM), moved, local).astype(BF16)
    for w in range(5):
        if w < 2:
            at, base, source, bias_at = WQ * w, WQ * w, kv, w
        else:
            at = pl.multiple_of(start + WQ * (w - 2), WQ)
            base, source, bias_at = WQ * (w - 2), local, last + (w - 4)
        rows, own = slice(base, base + WK), pl.ds(at, WQ)
        out = attend_window(
            q[own, :], source[rows, :AW], source[rows, AW:], bias[bias_at], at - LEFT_RIM, low,
            high,
        )
        gated[own, :] = (out * sigmoid(gate_in[own, :].astype(F32))).astype(BF16)
    mid = (x[...].astype(F32) + mm(gated[...], proj[...])).astype(BF16)
    live = lax.broadcasted_iota(jnp.int32, (atoms, AW), 0) < count
    mid_out[...] = jnp.where(live, mid, jnp.zeros_like(mid))
    lifted = jnp.maximum(mm(mid, lift[...]), 0.0).astype(BF16)
    member = jnp.where(membership(tok[...], count, tokens), 1.0, 0.0)
    summed = mm(member.astype(BF16), lifted)
    counts = jnp.sum(member, axis=1, keepdims=True)
    hidden = tsingle[...].astype(F32) + summed / counts
    hidden_out[...] = hidden
    normed_out[...] = normalise(hidden, tgain[...])


def head_windows():
    windows = []
    h = 0
    while h < TH:
        first = h * TD // 128 * 128
        first = min(first, TW - 256)
        heads = []
        while h < TH and (h + 1) * TD <= first + 256:
            heads.append(h)
            h += 1
        windows.append((first, heads))
    return windows


def query_body(info, normed, tok, qg, out, member_out, normed_out):
    tokens = normed.shape[0]
    count = info[lax.axis_index("row")]
    member = membership(tok[...], count, tokens)
    r = lax.broadcasted_iota(jnp.int32, (tokens, 3 * tokens), 0)
    c = lax.broadcasted_iota(jnp.int32, (tokens, 3 * tokens), 1)
    same = (c == r) | (c == r + tokens) | (c == r + 2 * tokens)
    one = jnp.where(member, 1.0, 0.0).astype(BF16)
    member_out[...] = mm_tn(one, jnp.where(same, 1.0, 0.0).astype(BF16)).astype(BF16)
    normed_out[...] = normed[...]
    out[...] = mm(normed[...], qg[...]).astype(BF16)


def token_body(offsets, begins, ends, *refs):
    number = len(offsets)
    own, oth, refs = refs[:number], refs[number : 2 * number], refs[2 * number :]
    query_gate, kv, bias, *refs = refs
    if not begins:
        st_in, acc_in, *refs = refs
    if ends:
        hidden_in, base, member, proj, down, atom_out, token_out, *refs = refs
        xs, kvs, qs, result, sems = refs
    else:
        st_out, acc_out, *refs = refs
        xs, kvs, qs = refs
    row = lax.axis_index("row")
    chip, core = row // 2, row % 2
    tokens = own[0].shape[0]
    pair = 2 * tokens
    keys = number * pair
    for j in range(number):
        at = pl.multiple_of(j * pair + core * tokens, tokens)
        xs[pl.ds(at, tokens), :] = own[j][...]
        at = pl.multiple_of(j * pair + (1 - core) * tokens, tokens)
        xs[pl.ds(at, tokens), :] = oth[j][...]
    column = lax.broadcasted_iota(jnp.int32, (tokens, 256), 1)
    windows = head_windows()
    for first, heads in windows:
        q = query_gate[:, first : first + 256]
        for h in heads:
            keep = (column >= h * TD - first) & (column < (h + 1) * TD - first)
            qs[h * tokens : (h + 1) * tokens, :] = jnp.where(keep, q, jnp.zeros_like(q))
    kvs[...] = mm(xs[...], kv[...]).astype(BF16)
    places = [pl.multiple_of((chip ^ offset) * pair, pair) for offset in offsets]
    pieces = [jnp.zeros((tokens, 128), F32) for _ in range(TW // 128)]
    tile_column = lax.broadcasted_iota(jnp.int32, (tokens, 128), 1)
    key_column = lax.broadcasted_iota(jnp.int32, (keys, 256), 1)
    for first, heads in windows:
        rows = slice(heads[0] * tokens, (heads[-1] + 1) * tokens)
        used = (heads[0] * TD - first, (heads[-1] + 1) * TD - first)
        spare = 255 if used[1] < 256 else 0
        scores = mm_nt(qs[rows, :], kvs[:, first : first + 256]) * TD ** (-0.5)
        tile = jnp.concatenate(
            [
                bias[heads[0] : heads[-1] + 1, :, pl.ds(at, pair)].reshape(-1, pair)
                for at in places
            ],
            axis=1,
        )
        scores = scores + tile.astype(F32)
        best = jnp.broadcast_to(jnp.max(scores, axis=-1, keepdims=True), (scores.shape[0], 128))
        if not begins:
            best = jnp.maximum(best, st_in[rows, :])
        raised = jnp.concatenate(
            [
                jnp.exp(scores[:, i : i + 128] - best).astype(BF16)
                for i in range(0, keys, 128)
            ],
            axis=1,
        )
        values = kvs[:, TW + first : TW + first + 256]
        values = jnp.where(
            (key_column >= used[0]) & (key_column < used[1]), values, jnp.ones_like(values)
        )
        mixed = mm(raised, values)
        if not begins:
            factor = jnp.exp(st_in[rows, :] - best)
            mixed = mixed + jnp.concatenate([factor, factor], axis=1) * acc_in[rows, :]
        if not ends:
            st_out[rows, :] = best
            acc_out[rows, :] = mixed
            continue
        inverse = 1.0 / mixed[:, spare : spare + 1]
        for i, h in enumerate(heads):
            part = slice(i * tokens, (i + 1) * tokens)
            for half in range(2):
                t = first // 128 + half
                a, b = h * TD - t * 128, (h + 1) * TD - t * 128
                if b <= 0 or a >= 128:
                    continue
                keep = (tile_column >= a) & (tile_column < b)
                value = mixed[part, half * 128 : (half + 1) * 128] * inverse[part]
                pieces[t] = jnp.where(keep, value, pieces[t])
    if not ends:
        return
    attended = jnp.concatenate(pieces, axis=1)
    gated = (attended * sigmoid(query_gate[:, TW:].astype(F32))).astype(BF16)
    final = (hidden_in[...] + mm(gated, proj[...])).astype(BF16)
    result[...] = final
    store = pltpu.make_async_copy(result, token_out, sems.at[0])
    store.start()
    back = mm(final, down[...])
    high = back.astype(BF16)
    rest = back - high.astype(F32)
    low = rest.astype(BF16)
    lowest = (rest - low.astype(F32)).astype(BF16)
    spread = mm(member[...], jnp.concatenate([high, low, lowest], axis=0))
    atom_out[...] = (base[...].astype(F32) + spread).astype(BF16)
    store.wait()


def vmem(count):
    return [pl.BlockSpec(memory_space=VMEM) for _ in range(count)]


def anywhere(count):
    return [pl.BlockSpec(memory_space=pltpu.HBM) for _ in range(count)]


def scalars():
    return [pl.BlockSpec(memory_space=SMEM)]


def like(shape, dtype):
    return jax.ShapeDtypeStruct(shape, dtype)


def solution(mesh):
    width = mesh.shape["row"]
    nchip = width // 2
    groups = [list(range(k, min(k + 4, nchip))) for k in range(0, nchip, 4)]
    if nchip == 8:
        groups = [[0, 1, 2, 4], [3, 5, 6, 7]]

    def swap(value, bits):
        return lax.ppermute(value, "row", [(i, i ^ bits) for i in range(width)])

    def on_device(
        atom_single, atom_count, atom_token, atom_bias, token_single, token_bias, atom_gain,
        atom_qkvg, atom_proj, atom_to_token, token_gain, token_qg, token_kv, token_proj,
        token_to_atom,
    ):
        atoms = atom_single.shape[0]
        tokens = token_single.shape[0]
        rows = LEFT_RIM + atoms + RIGHT_RIM
        far = lax.ppermute(
            atom_single, "row",
            [(i, i + 1 if i % 2 else i - 1) for i in range(1, width - 1)],
        )
        near = swap(atom_single, 1)
        tok = atom_token.reshape(1, atoms)
        gain = atom_gain.reshape(1, AW)
        q, kv, gate, gated = pl.pallas_call(
            early_body,
            out_shape=(
                like((atoms, AW), BF16), like((rows, 2 * AW), BF16), like((atoms, AW), BF16),
                like((atoms, AW), BF16),
            ),
            in_specs=scalars() + vmem(4),
            out_specs=tuple(vmem(4)),
            compiler_params=pltpu.CompilerParams(vmem_limit_bytes=59200 << 10),
            name="early",
        )(atom_count, atom_single, atom_bias, gain, atom_qkvg)
        normed, hidden, mid = pl.pallas_call(
            late_body,
            out_shape=(like((tokens, TW), BF16), like((tokens, TW), F32), like((atoms, AW), BF16)),
            in_specs=scalars() + vmem(15),
            out_specs=tuple(vmem(3)),
            scratch_shapes=[VMEM((rows, 2 * AW), BF16), VMEM((atoms, AW), BF16)],
            compiler_params=pltpu.CompilerParams(vmem_limit_bytes=59200 << 10),
            name="late",
        )(
            atom_count, near, far, q, kv, gate, gated, tok, gain, token_gain, atom_bias,
            atom_qkvg, atom_single, atom_proj, atom_to_token, token_single,
        )
        blocks, other = {0: normed}, {}
        for k in range(1, nchip):
            top = 1 << (k.bit_length() - 1)
            direct = k == top or k < 4
            blocks[k] = swap(normed if direct else blocks[top], 2 * (k if direct else k ^ top))
        for k in range(nchip):
            other[k] = swap(blocks[k], 1)
        query_gate, member, normed_again = pl.pallas_call(
            query_body,
            out_shape=(
                like((tokens, 2 * TW), BF16), like((atoms, 3 * tokens), BF16),
                like((tokens, TW), BF16),
            ),
            in_specs=scalars() + vmem(3),
            out_specs=tuple(vmem(3)),
            compiler_params=pltpu.CompilerParams(vmem_limit_bytes=8 << 20),
            name="queries",
        )(atom_count, normed, tok, token_qg)
        blocks[0] = normed_again
        state = ()
        for offsets in groups:
            begin = offsets[0]
            begins, ends = begin == 0, offsets[-1] == nchip - 1
            number = len(offsets)
            keys = number * 2 * tokens
            arrays = [blocks[k] for k in offsets] + [other[k] for k in offsets]
            arrays += [query_gate, token_kv, token_bias, *state]
            specs = vmem(2 * number + 3 + len(state))
            scratch = [
                VMEM((keys, TW), BF16), VMEM((keys, 2 * TW), BF16), VMEM((TH * tokens, 256), BF16),
            ]
            if ends:
                arrays += [hidden, mid, member, token_proj, token_to_atom]
                specs += vmem(5)
                outs = (like((atoms, AW), BF16), like((tokens, TW), BF16))
                scratch += [VMEM((tokens, TW), BF16), pltpu.SemaphoreType.DMA((1,))]
            else:
                outs = (like((TH * tokens, 128), F32), like((TH * tokens, 256), F32))
            state = pl.pallas_call(
                lambda *refs: token_body(offsets, begins, ends, *refs),
                out_shape=outs,
                in_specs=specs,
                out_specs=tuple(vmem(1) + (anywhere(1) if ends else vmem(1))),
                scratch_shapes=scratch,
                compiler_params=pltpu.CompilerParams(vmem_limit_bytes=16 << 20),
            )(*arrays)
        return state

    split = P(("sample", "row"), None)
    return jax.shard_map(
        on_device,
        mesh=mesh,
        in_specs=(
            split, P(), P("row"), P("row", None, None, None), split, P(None, "row", None),
            P(), P(), P(), P(), P(), P(), P(), P(), P(),
        ),
        out_specs=(split, split),
        check_vma=False,
    )
```

```python
import jax
import jax.numpy as jnp
from jax import lax
from jax.experimental import pallas as pl
from jax.experimental.pallas import tpu as pltpu
from jax.sharding import PartitionSpec as P


TW = 768
TH = 16
AW = 128
AH = 4
WQ = 32
WK = 128
LEFT_RIM = 48
RIGHT_RIM = 80
AD = AW // AH
TD = TW // TH

EPSILON = 1e-05
MASKED = -1000000000.0
F32 = jnp.float32
BF16 = jnp.bfloat16
VMEM = pltpu.VMEM
SMEM = pltpu.SMEM


def mm(a, b):
    return lax.dot_general(a, b, (((1,), (0,)), ((), ())), preferred_element_type=F32)


def mm_nt(a, b):
    return lax.dot_general(a, b, (((1,), (1,)), ((), ())), preferred_element_type=F32)


def mm_tn(a, b):
    return lax.dot_general(a, b, (((0,), (0,)), ((), ())), preferred_element_type=F32)


def normalise(values, gain):
    average = jnp.mean(values, axis=-1, keepdims=True)
    centred = values - average
    spread = jnp.mean(centred * centred, axis=-1, keepdims=True)
    return (centred * lax.rsqrt(spread + EPSILON) * gain).astype(BF16)


def sigmoid(values):
    return 1.0 / (1.0 + jnp.exp(-values))


def membership(tok, count, tokens):
    atoms = tok.shape[1]
    slot = lax.broadcasted_iota(jnp.int32, (tokens, atoms), 1)
    name = lax.broadcasted_iota(jnp.int32, (tokens, atoms), 0)
    return (tok == name) & (slot < count)


def attend_window(q, k, v, bias, first, low, high):
    lane = lax.broadcasted_iota(jnp.int32, (WQ, AW), 1) // AD
    spread_q = jnp.concatenate(
        [jnp.where(lane == h, q, jnp.zeros_like(q)) for h in range(AH)], axis=0
    )
    scores = mm_nt(spread_q, k) * AD ** (-0.5)
    scores = scores + bias.reshape(AH * WQ, WK).astype(F32)
    p = lax.broadcasted_iota(jnp.int32, (1, WK), 1) + first
    scores = jnp.where((p >= low) & (p < high), scores, MASKED)
    raised = jnp.exp(scores - jnp.max(scores, axis=-1, keepdims=True))
    both = mm(raised.astype(BF16), jnp.concatenate([v, jnp.ones_like(v)], axis=1))
    mixed = both[:, :AW] / both[:, AW:]
    out = jnp.zeros((WQ, AW), F32)
    for h in range(AH):
        out = jnp.where(lane == h, mixed[WQ * h : WQ * (h + 1)], out)
    return out


def early_body(
    info, x, bias, gain, qkvg, kv_out, gated_out, q_some, gate_some, bias_some, q_out, gate_out
):
    row = lax.axis_index("row")
    count = info[row]
    atoms = x.shape[0]
    normed = normalise(x[...].astype(F32), gain[...])
    parts = mm(normed, qkvg[...]).astype(BF16)
    q_out[...] = parts[:, :AW]
    gate_out[...] = parts[:, 3 * AW :]
    kv_out[0:LEFT_RIM, :] = jnp.zeros((LEFT_RIM, 2 * AW), BF16)
    kv_out[LEFT_RIM : LEFT_RIM + atoms, :] = parts[:, AW : 3 * AW]
    kv_out[LEFT_RIM + atoms :, :] = jnp.zeros((RIGHT_RIM, 2 * AW), BF16)
    for w in range(atoms // WQ):
        rows = slice(WQ * w, WQ * w + WK)
        own = slice(WQ * w, WQ * (w + 1))
        out = attend_window(
            q_out[own, :], kv_out[rows, :AW], kv_out[rows, AW:],
            bias[w], WQ * w - LEFT_RIM, 0, count,
        )
        gated_out[own, :] = (out * sigmoid(gate_out[own, :].astype(F32))).astype(BF16)
    last = (count - 1) // WQ
    for w in range(5):
        place = w if w < 2 else last + (w - 4)
        own, to = pl.ds(pl.multiple_of(place * WQ, WQ), WQ), slice(WQ * w, WQ * (w + 1))
        q_some[to, :] = q_out[own, :]
        gate_some[to, :] = gate_out[own, :]
        bias_some[w] = bias[place]


def late_body(
    info, near, far, q, kv_in, gate_in, gated_in, tok, gain, tgain, bias, qkvg, x, proj, lift,
    tsingle, normed_out, hidden_out, mid_out, kv, gated,
):
    row = lax.axis_index("row")
    width = lax.axis_size("row")
    count = info[row]
    atoms = x.shape[0]
    tokens = tsingle.shape[0]
    last = (count - 1) // WQ
    odd = row % 2 == 1
    previous = jnp.where(odd, near[...], far[...])
    following = jnp.where(odd, far[0:RIGHT_RIM, :], near[0:RIGHT_RIM, :])
    before_count = info[jnp.maximum(row - 1, 0)]
    r = lax.broadcasted_iota(jnp.int32, (LEFT_RIM, atoms), 0) + (before_count - LEFT_RIM)
    pick = r == lax.broadcasted_iota(jnp.int32, (LEFT_RIM, atoms), 1)
    before = mm(jnp.where(pick, 1.0, 0.0).astype(BF16), previous)
    rims = jnp.concatenate([before, following.astype(F32)], axis=0)
    rim_kv = mm(normalise(rims, gain[...]), qkvg[:, AW : 3 * AW]).astype(BF16)
    after_kv = rim_kv[LEFT_RIM:]
    kv[...] = kv_in[...]
    kv[0:LEFT_RIM, :] = rim_kv[:LEFT_RIM]
    gated[...] = gated_in[...]
    low = jnp.where(row == 0, 0, -4 * atoms)
    high = jnp.where(row == width - 1, count, 4 * atoms)
    region = 2 * WQ + WK
    start = pl.multiple_of((last - 2) * WQ, WQ)
    r = lax.broadcasted_iota(jnp.int32, (region, RIGHT_RIM), 0) + (start - LEFT_RIM - count)
    pick = r == lax.broadcasted_iota(jnp.int32, (region, RIGHT_RIM), 1)
    moved = mm(jnp.where(pick, 1.0, 0.0).astype(BF16), after_kv)
    r = lax.broadcasted_iota(jnp.int32, (region, 2 * AW), 0) + (start - LEFT_RIM - count)
    local = kv[pl.ds(start, region), :].astype(F32)
    local = jnp.where((r >= 0) & (r < RIGHT_RIM), moved, local).astype(BF16)
    for w in range(5):
        if w < 2:
            at, base, source = WQ * w, WQ * w, kv
        else:
            at = pl.multiple_of(start + WQ * (w - 2), WQ)
            base, source = WQ * (w - 2), local
        rows, own, to = slice(base, base + WK), pl.ds(at, WQ), slice(WQ * w, WQ * (w + 1))
        out = attend_window(
            q[to, :], source[rows, :AW], source[rows, AW:], bias[w], at - LEFT_RIM, low, high,
        )
        gated[own, :] = (out * sigmoid(gate_in[to, :].astype(F32))).astype(BF16)
    mid = (x[...].astype(F32) + mm(gated[...], proj[...])).astype(BF16)
    live = lax.broadcasted_iota(jnp.int32, (atoms, AW), 0) < count
    mid_out[...] = jnp.where(live, mid, jnp.zeros_like(mid))
    lifted = jnp.maximum(mm(mid, lift[...]), 0.0).astype(BF16)
    member = jnp.where(membership(tok[...], count, tokens), 1.0, 0.0)
    summed = mm(member.astype(BF16), lifted)
    counts = jnp.sum(member, axis=1, keepdims=True)
    hidden = tsingle[...].astype(F32) + summed / counts
    hidden_out[...] = hidden
    normed_out[...] = normalise(hidden, tgain[...])


def head_windows():
    windows = []
    h = 0
    while h < TH:
        first = h * TD // 128 * 128
        first = min(first, TW - 256)
        heads = []
        while h < TH and (h + 1) * TD <= first + 256:
            heads.append(h)
            h += 1
        windows.append((first, heads))
    return windows


def query_body(info, normed, tok, qg, out, member_out, normed_out):
    tokens = normed.shape[0]
    count = info[lax.axis_index("row")]
    member = membership(tok[...], count, tokens)
    r = lax.broadcasted_iota(jnp.int32, (tokens, 3 * tokens), 0)
    c = lax.broadcasted_iota(jnp.int32, (tokens, 3 * tokens), 1)
    same = (c == r) | (c == r + tokens) | (c == r + 2 * tokens)
    one = jnp.where(member, 1.0, 0.0).astype(BF16)
    member_out[...] = mm_tn(one, jnp.where(same, 1.0, 0.0).astype(BF16)).astype(BF16)
    normed_out[...] = normed[...]
    out[...] = mm(normed[...], qg[...]).astype(BF16)


def token_body(offsets, begins, ends, *refs):
    number = len(offsets)
    own, oth, refs = refs[:number], refs[number : 2 * number], refs[2 * number :]
    query_gate, kv, bias, *refs = refs
    if not begins:
        st_in, acc_in, *refs = refs
    if ends:
        hidden_in, base, member, proj, down, atom_out, token_out, *refs = refs
        xs, kvs, qs, result, sems = refs
    else:
        st_out, acc_out, *refs = refs
        xs, kvs, qs = refs
    row = lax.axis_index("row")
    chip, core = row // 2, row % 2
    tokens = own[0].shape[0]
    pair = 2 * tokens
    keys = number * pair
    for j in range(number):
        at = pl.multiple_of(j * pair + core * tokens, tokens)
        xs[pl.ds(at, tokens), :] = own[j][...]
        at = pl.multiple_of(j * pair + (1 - core) * tokens, tokens)
        xs[pl.ds(at, tokens), :] = oth[j][...]
    column = lax.broadcasted_iota(jnp.int32, (tokens, 256), 1)
    windows = head_windows()
    for first, heads in windows:
        q = query_gate[:, first : first + 256]
        for h in heads:
            keep = (column >= h * TD - first) & (column < (h + 1) * TD - first)
            qs[h * tokens : (h + 1) * tokens, :] = jnp.where(keep, q, jnp.zeros_like(q))
    kvs[...] = mm(xs[...], kv[...]).astype(BF16)
    places = [pl.multiple_of((chip ^ offset) * pair, pair) for offset in offsets]
    pieces = [jnp.zeros((tokens, 128), F32) for _ in range(TW // 128)]
    tile_column = lax.broadcasted_iota(jnp.int32, (tokens, 128), 1)
    key_column = lax.broadcasted_iota(jnp.int32, (keys, 256), 1)
    for first, heads in windows:
        rows = slice(heads[0] * tokens, (heads[-1] + 1) * tokens)
        used = (heads[0] * TD - first, (heads[-1] + 1) * TD - first)
        spare = 255 if used[1] < 256 else 0
        scores = mm_nt(qs[rows, :], kvs[:, first : first + 256]) * TD ** (-0.5)
        tile = jnp.concatenate(
            [
                bias[heads[0] : heads[-1] + 1, :, pl.ds(at, pair)].reshape(-1, pair)
                for at in places
            ],
            axis=1,
        )
        scores = scores + tile.astype(F32)
        best = jnp.broadcast_to(jnp.max(scores, axis=-1, keepdims=True), (scores.shape[0], 128))
        if not begins:
            best = jnp.maximum(best, st_in[rows, :])
        raised = jnp.concatenate(
            [
                jnp.exp(scores[:, i : i + 128] - best).astype(BF16)
                for i in range(0, keys, 128)
            ],
            axis=1,
        )
        values = kvs[:, TW + first : TW + first + 256]
        values = jnp.where(
            (key_column >= used[0]) & (key_column < used[1]), values, jnp.ones_like(values)
        )
        mixed = mm(raised, values)
        if not begins:
            factor = jnp.exp(st_in[rows, :] - best)
            mixed = mixed + jnp.concatenate([factor, factor], axis=1) * acc_in[rows, :]
        if not ends:
            st_out[rows, :] = best
            acc_out[rows, :] = mixed
            continue
        inverse = 1.0 / mixed[:, spare : spare + 1]
        for i, h in enumerate(heads):
            part = slice(i * tokens, (i + 1) * tokens)
            for half in range(2):
                t = first // 128 + half
                a, b = h * TD - t * 128, (h + 1) * TD - t * 128
                if b <= 0 or a >= 128:
                    continue
                keep = (tile_column >= a) & (tile_column < b)
                value = mixed[part, half * 128 : (half + 1) * 128] * inverse[part]
                pieces[t] = jnp.where(keep, value, pieces[t])
    if not ends:
        return
    attended = jnp.concatenate(pieces, axis=1)
    gated = (attended * sigmoid(query_gate[:, TW:].astype(F32))).astype(BF16)
    final = (hidden_in[...] + mm(gated, proj[...])).astype(BF16)
    result[...] = final
    store = pltpu.make_async_copy(result, token_out, sems.at[0])
    store.start()
    back = mm(final, down[...])
    high = back.astype(BF16)
    rest = back - high.astype(F32)
    low = rest.astype(BF16)
    lowest = (rest - low.astype(F32)).astype(BF16)
    spread = mm(member[...], jnp.concatenate([high, low, lowest], axis=0))
    atom_out[...] = (base[...].astype(F32) + spread).astype(BF16)
    store.wait()


def vmem(count):
    return [pl.BlockSpec(memory_space=VMEM) for _ in range(count)]


def anywhere(count):
    return [pl.BlockSpec(memory_space=pltpu.HBM) for _ in range(count)]


def scalars():
    return [pl.BlockSpec(memory_space=SMEM)]


def like(shape, dtype):
    return jax.ShapeDtypeStruct(shape, dtype)


def solution(mesh):
    width = mesh.shape["row"]
    nchip = width // 2
    groups = [list(range(k, min(k + 4, nchip))) for k in range(0, nchip, 4)]
    if nchip == 8:
        groups = [[0, 1, 2, 4], [3, 5, 6, 7]]

    def swap(value, bits):
        return lax.ppermute(value, "row", [(i, i ^ bits) for i in range(width)])

    def on_device(
        atom_single, atom_count, atom_token, atom_bias, token_single, token_bias, atom_gain,
        atom_qkvg, atom_proj, atom_to_token, token_gain, token_qg, token_kv, token_proj,
        token_to_atom,
    ):
        atoms = atom_single.shape[0]
        tokens = token_single.shape[0]
        rows = LEFT_RIM + atoms + RIGHT_RIM
        far = lax.ppermute(
            atom_single, "row",
            [(i, i + 1 if i % 2 else i - 1) for i in range(1, width - 1)],
        )
        near = swap(atom_single, 1)
        tok = atom_token.reshape(1, atoms)
        gain = atom_gain.reshape(1, AW)
        kv, gated, q, gate, some = pl.pallas_call(
            early_body,
            out_shape=(
                like((rows, 2 * AW), BF16), like((atoms, AW), BF16), like((5 * WQ, AW), BF16),
                like((5 * WQ, AW), BF16), like((5, AH, WQ, WK), BF16),
            ),
            in_specs=scalars() + vmem(4),
            out_specs=tuple(vmem(5)),
            scratch_shapes=[VMEM((atoms, AW), BF16), VMEM((atoms, AW), BF16)],
            compiler_params=pltpu.CompilerParams(vmem_limit_bytes=59200 << 10),
            name="early",
        )(atom_count, atom_single, atom_bias, gain, atom_qkvg)
        normed, hidden, mid = pl.pallas_call(
            late_body,
            out_shape=(like((tokens, TW), BF16), like((tokens, TW), F32), like((atoms, AW), BF16)),
            in_specs=scalars() + vmem(15),
            out_specs=tuple(vmem(3)),
            scratch_shapes=[VMEM((rows, 2 * AW), BF16), VMEM((atoms, AW), BF16)],
            compiler_params=pltpu.CompilerParams(vmem_limit_bytes=59200 << 10),
            name="late",
        )(
            atom_count, near, far, q, kv, gate, gated, tok, gain, token_gain, some,
            atom_qkvg, atom_single, atom_proj, atom_to_token, token_single,
        )
        blocks, other = {0: normed}, {}
        for k in range(1, nchip):
            top = 1 << (k.bit_length() - 1)
            direct = k == top or k < 4
            blocks[k] = swap(normed if direct else blocks[top], 2 * (k if direct else k ^ top))
        for k in range(nchip):
            other[k] = swap(blocks[k], 1)
        query_gate, member, normed_again = pl.pallas_call(
            query_body,
            out_shape=(
                like((tokens, 2 * TW), BF16), like((atoms, 3 * tokens), BF16),
                like((tokens, TW), BF16),
            ),
            in_specs=scalars() + vmem(3),
            out_specs=tuple(vmem(3)),
            compiler_params=pltpu.CompilerParams(vmem_limit_bytes=8 << 20),
            name="queries",
        )(atom_count, normed, tok, token_qg)
        blocks[0] = normed_again
        state = ()
        for offsets in groups:
            begin = offsets[0]
            begins, ends = begin == 0, offsets[-1] == nchip - 1
            number = len(offsets)
            keys = number * 2 * tokens
            arrays = [blocks[k] for k in offsets] + [other[k] for k in offsets]
            arrays += [query_gate, token_kv, token_bias, *state]
            specs = vmem(2 * number + 3 + len(state))
            scratch = [
                VMEM((keys, TW), BF16), VMEM((keys, 2 * TW), BF16), VMEM((TH * tokens, 256), BF16),
            ]
            if ends:
                arrays += [hidden, mid, member, token_proj, token_to_atom]
                specs += vmem(5)
                outs = (like((atoms, AW), BF16), like((tokens, TW), BF16))
                scratch += [VMEM((tokens, TW), BF16), pltpu.SemaphoreType.DMA((1,))]
            else:
                outs = (like((TH * tokens, 128), F32), like((TH * tokens, 256), F32))
            state = pl.pallas_call(
                lambda *refs: token_body(offsets, begins, ends, *refs),
                out_shape=outs,
                in_specs=specs,
                out_specs=tuple(vmem(1) + (anywhere(1) if ends else vmem(1))),
                scratch_shapes=scratch,
                compiler_params=pltpu.CompilerParams(vmem_limit_bytes=16 << 20),
            )(*arrays)
        return state

    split = P(("sample", "row"), None)
    return jax.shard_map(
        on_device,
        mesh=mesh,
        in_specs=(
            split, P(), P("row"), P("row", None, None, None), split, P(None, "row", None),
            P(), P(), P(), P(), P(), P(), P(), P(), P(),
        ),
        out_specs=(split, split),
        check_vma=False,
    )
```
